128 devices in a mesh: space: 16 (over y_hi, x, core), code: 4 (over z), clip: 2 (over y_lo).
Axes of the slice: x: 4, y: 4 (y_hi: 2, y_lo: 2; y = y_hi * 2 + y_lo), z: 4, core: 2. Of those that a mesh axis runs over, the one named last changes fastest.
Arguments:
- soft_weights: bfloat16 [2, 1024, 32, 8192], P('clip', 'space', None, 'code'), may hold values from 0.00029945374 to 0.029907227
- codebook: bfloat16 [8192, 256], P('code'), may hold values from -6 to 6
- kernel_one: bfloat16 [3, 3, 256, 512], replicated, may hold values from -0.125 to 0.125
- kernel_two: bfloat16 [3, 3, 512, 512], replicated, may hold values from -0.09375 to 0.09375
- cotangent: bfloat16 [2, 1024, 32, 512], P('clip', ('space', 'code')), may hold values from -16 to 16
Outputs:
- decoded: bfloat16 [2, 1024, 32, 512], P('clip', ('space', 'code'))
- grad_one: float32 [3, 3, 256, 512], P(None, None, None, ('space', 'code', 'clip'))
- grad_two: float32 [3, 3, 512, 512], P(None, None, None, ('space', 'code', 'clip'))
- grad_codebook: float32 [8192, 256], P('code')
The draws below stay inside these ranges and needn't reach their ends.
All inputs are finite; a program needn't handle non-finite values.
Results may differ from the reference program's by a relative error of at most 0.02.
Values may be sent and summed in bfloat16 or wider, within the bound.
A program may use at most 192 MiB of HBM per device.

```python
import math
import jax
import jax.numpy as jnp
from jax import lax

CODES = 8192
CH = 256
WIDTH = 512
COLS = 32
ROWS = 1024
CLIPS = 2
N_CLIP = 2


def spiked(drawn, stream_key, source, target, parts, factor):
    owner, partner = [(jnp.arange(drawn.shape[axis_at]) // (drawn.shape[axis_at] // parts)).reshape([-1 if axis == axis_at else 1 for axis in range(drawn.ndim)]) for axis_at in (source, target)]
    chosen = jax.random.permutation(stream_key, parts)[partner]
    strong = (owner == chosen) | (owner == (partner + parts // 2) % parts)
    return jnp.where(strong, factor * drawn, drawn)


def shard_levels(own_key, extent, cuts, low, high):
    loudness = 1.0
    for dim, shards_of in cuts:
        heights = jax.random.uniform(jax.random.fold_in(jax.random.fold_in(own_key, 6), dim), (shards_of,), jnp.float32, low / len(cuts), high / len(cuts))
        loudness = loudness * jnp.repeat(jnp.exp(heights), extent[dim] // shards_of).reshape((-1,) + (1,) * (len(extent) - 1 - dim))
    return loudness


def normal_values(stream_key, extent, scale, most, split=(), kind=jnp.bfloat16):
    factor_of = shard_levels(stream_key, extent, split, -0.22, 0.18) if split else 1.0
    array = jax.random.normal(stream_key, extent, jnp.float32) * scale * factor_of
    return jnp.minimum(jnp.maximum(array, -most), most).astype(kind)


def noise_with(rng, shape, scale, bound, shards, heavy, dtype=jnp.bfloat16):
    values = scale * jax.random.normal(rng, shape, jnp.float32)
    if shards:
        values = values * shard_levels(rng, shape, shards, -0.22, 0.18)
    return jnp.clip(spiked(values, jax.random.fold_in(rng, 3), *heavy), -bound, bound).astype(dtype)


def setup_inputs(seed: int = 0) -> dict:
    splits = jax.random.split(jax.random.key(seed), 6)
    soft_weights = jnp.clip(jnp.exp(math.log(0.029907227) - 4.6038955 * jax.random.uniform(splits[0], (CLIPS, ROWS, COLS, CODES), jnp.float32) ** shard_levels(splits[0], (CLIPS, ROWS, COLS, CODES), ((0, 2), (1, 16), (3, 4)), -0.2, 0.2)), 0.00029945374, 0.029907227).astype(jnp.bfloat16)
    codebook = normal_values(splits[1], (CODES, CH), 1.0, 6.0, ((0, 4),))
    kernel_one = normal_values(splits[2], (3, 3, CH, WIDTH), (9 * CH) ** -0.5, 0.125)
    kernel_two = normal_values(splits[3], (3, 3, WIDTH, WIDTH), (9 * WIDTH) ** -0.5, 0.09375)
    cotangent = noise_with(splits[4], (CLIPS, ROWS, COLS, WIDTH), 1.0, 16.0, ((0, 2), (1, 64)), (1, 3, 64, 4.0))
    return {"soft_weights": soft_weights, "codebook": codebook, "kernel_one": kernel_one, "kernel_two": kernel_two, "cotangent": cotangent}


def pad_grid(field):
    return jnp.pad(field, ((1, 1), (1, 1), (0, 0)))

def taps_forward(padded, kernel):
    height = padded.shape[0] - 2
    breadth = padded.shape[1] - 2
    accum = jnp.zeros((height * breadth, kernel.shape[3]), jnp.float32)
    for first in range(3):
        for second in range(3):
            window = padded[first:first + height, second:second + breadth].reshape(height * breadth, -1)
            accum = accum + jnp.dot(window, kernel[first, second], preferred_element_type=jnp.float32)
    return accum.reshape(height, breadth, -1)

def taps_back(padded, kernel):
    height = padded.shape[0] - 2
    breadth = padded.shape[1] - 2
    accum = jnp.zeros((height * breadth, kernel.shape[2]), jnp.float32)
    for first in range(3):
        for second in range(3):
            window = padded[2 - first:2 - first + height, 2 - second:2 - second + breadth].reshape(height * breadth, -1)
            accum = accum + jnp.dot(window, kernel[first, second].T, preferred_element_type=jnp.float32)
    return accum.reshape(height, breadth, -1)

def kernel_grad(padded, upstream):
    height = upstream.shape[0]
    breadth = upstream.shape[1]
    flat_up = upstream.reshape(height * breadth, -1)
    result = []
    for first in range(3):
        line = []
        for second in range(3):
            window = padded[first:first + height, second:second + breadth].reshape(height * breadth, -1)
            line.append(lax.dot_general(window, flat_up, (((0,), (0,)), ((), ())), preferred_element_type=jnp.float32))
        result.append(jnp.stack(line))
    return jnp.stack(result)

def reference(soft_weights, codebook, kernel_one, kernel_two, cotangent):
    outputs = []
    grad_one = jnp.zeros(kernel_one.shape, jnp.float32)
    grad_two = jnp.zeros(kernel_two.shape, jnp.float32)
    grad_codebook = jnp.zeros(codebook.shape, jnp.float32)
    for clip_index in range(N_CLIP):
        flat = soft_weights[clip_index].reshape(-1, CODES)
        embedded = jnp.dot(flat, codebook, preferred_element_type=jnp.float32).reshape(ROWS, COLS, CH).astype(jnp.bfloat16)
        embed_pad = pad_grid(embedded)
        pre_one = taps_forward(embed_pad, kernel_one)
        hidden = jax.nn.silu(pre_one).astype(jnp.bfloat16)
        hidden_pad = pad_grid(hidden)
        outputs.append(taps_forward(hidden_pad, kernel_two).astype(jnp.bfloat16))
        upstream = cotangent[clip_index]
        grad_two = grad_two + kernel_grad(hidden_pad, upstream)
        grad_hidden = taps_back(pad_grid(upstream), kernel_two)
        sigma = jax.nn.sigmoid(pre_one)
        grad_pre = (grad_hidden * sigma * (1.0 + pre_one * (1.0 - sigma))).astype(jnp.bfloat16)
        grad_one = grad_one + kernel_grad(embed_pad, grad_pre)
        grad_embedded = taps_back(pad_grid(grad_pre), kernel_one).astype(jnp.bfloat16)
        grad_codebook = grad_codebook + lax.dot_general(flat, grad_embedded.reshape(-1, CH), (((0,), (0,)), ((), ())), preferred_element_type=jnp.float32)
    return (jnp.stack(outputs), grad_one, grad_two, grad_codebook)
```

```python
import functools

import jax
import jax.numpy as jnp
from jax import lax
from jax.experimental import pallas as pl
from jax.experimental.pallas import tpu as pltpu
from jax.sharding import PartitionSpec as P

MESH = pl.DeviceIdType.MESH
F32 = jnp.float32
BF16 = jnp.bfloat16
COLS = 32
COLOURS = 6


def dot(a, b):
    return jnp.dot(a, b, preferred_element_type=F32)


def dot_nt(a, b):
    return lax.dot_general(a, b, (((1,), (1,)), ((), ())), preferred_element_type=F32)


def rem(a, b):
    return lax.rem(a, jnp.int32(b))


def div(a, b):
    return lax.div(a, jnp.int32(b))


def coords():
    space = lax.axis_index("space")
    return {
        "core": rem(space, 2),
        "x": rem(div(space, 2), 4),
        "y_hi": div(space, 8),
        "z": lax.axis_index("code"),
        "y_lo": lax.axis_index("clip"),
    }


def device(here, **moved):
    at = dict(here, **moved)
    return {
        "space": at["y_hi"] * 8 + at["x"] * 2 + at["core"],
        "code": at["z"],
        "clip": at["y_lo"],
    }


def flip(value):
    return value + 1 - 2 * rem(value, 2)


def links(here):
    y = here["y_hi"] * 2 + here["y_lo"]
    partners = [
        device(here, x=flip(here["x"])),
        device(here, x=3 - here["x"]),
        device(here, y_lo=1 - here["y_lo"]),
        device(here, y_hi=1 - here["y_hi"], y_lo=1 - here["y_lo"]),
        device(here, z=flip(here["z"])),
        device(here, z=3 - here["z"]),
    ]
    bits = []
    for at in (here["x"], y, here["z"]):
        bits += [rem(at + div(at, 2), 2), div(at, 2)]
    return partners, bits


class Wire:
    def __init__(self, send_sems, recv_sems):
        self.send_sems = send_sems
        self.recv_sems = recv_sems
        self.count = 0
        self.sent = []

    def copy(self, src, dst, to):
        made = pltpu.make_async_remote_copy(
            src_ref=src,
            dst_ref=dst,
            send_sem=self.send_sems.at[self.count],
            recv_sem=self.recv_sems.at[self.count],
            device_id=to,
            device_id_type=MESH,
        )
        self.count += 1
        made.start()
        self.sent.append(made)
        return made

    def drain(self):
        for made in self.sent:
            made.wait_send()


def greet(devices):
    barrier = pltpu.get_barrier_semaphore()
    for to in devices:
        pl.semaphore_signal(barrier, inc=1, device_id=to, device_id_type=MESH)
    pl.semaphore_wait(barrier, len(devices))


def front_kernel(
    w_hbm, book, cot, ext_e, ext_c,
    wbuf, keep_u, keep_v, keep_own, snd_a, snd_b, rcv_a, rcv_b, own, halo_e, halo_c,
    load_sem, send_sems, recv_sems,
):
    here = coords()
    z = here["z"]
    block = lax.axis_index("space") * 4 + z
    blocks = lax.axis_size("space") * 4
    cells = own.shape[0]
    half = book.shape[1] // 2
    edge = 2 * COLS
    zu, zv = flip(z), 3 - z
    order = [rem(z + 2, 4), zu, zv, z]
    loads = []
    for slot, chunk in enumerate(order):
        rows = pl.ds(pl.multiple_of(chunk * cells, cells), cells)
        load = pltpu.make_async_copy(w_hbm.at[rows], wbuf.at[slot], load_sem.at[slot])
        load.start()
        loads.append(load)

    def at_block(index):
        return {"space": div(index, 4), "code": rem(index, 4)}

    after, before = at_block(rem(block + 1, blocks)), at_block(rem(block + blocks - 1, blocks))
    to_u, to_v = device(here, z=zu), device(here, z=zv)
    greet([to_u, to_v, after, before])
    wire = Wire(send_sems, recv_sems)
    cot_down = wire.copy(cot.at[pl.ds(cells - edge, edge)], halo_c.at[0], after)
    cot_up = wire.copy(cot.at[pl.ds(0, edge)], halo_c.at[1], before)

    def partial(slot):
        loads[slot].wait()
        return dot(wbuf[slot], book[...])

    value = partial(0)
    snd_a[1] = value[:, :half].astype(BF16)
    snd_b[1] = value[:, half:].astype(BF16)
    far_a = wire.copy(snd_a.at[1], rcv_a.at[1], to_u)
    far_b = wire.copy(snd_b.at[1], rcv_b.at[1], to_v)
    value = partial(1)
    snd_a[0] = value[:, :half].astype(BF16)
    near_a = wire.copy(snd_a.at[0], rcv_a.at[0], to_u)
    keep_u[...] = value[:, half:]
    value = partial(2)
    snd_b[0] = value[:, half:].astype(BF16)
    near_b = wire.copy(snd_b.at[0], rcv_b.at[0], to_v)
    keep_v[...] = value[:, :half]
    keep_own[...] = partial(3)
    far_a.wait_recv()
    snd_a[2] = (keep_v[...] + rcv_a[1].astype(F32)).astype(BF16)
    last_a = wire.copy(snd_a.at[2], rcv_a.at[2], to_v)
    far_b.wait_recv()
    snd_b[2] = (keep_u[...] + rcv_b[1].astype(F32)).astype(BF16)
    last_b = wire.copy(snd_b.at[2], rcv_b.at[2], to_u)
    cot_down.wait_recv()
    cot_up.wait_recv()
    zero_c = jnp.zeros((edge, cot.shape[1]), BF16)
    ext_c[pl.ds(0, edge)] = jnp.where(block == 0, zero_c, halo_c[0])
    ext_c[pl.ds(edge, cells)] = cot[...]
    ext_c[pl.ds(edge + cells, edge)] = jnp.where(block == blocks - 1, zero_c, halo_c[1])
    near_a.wait_recv()
    near_b.wait_recv()
    last_a.wait_recv()
    own[:, :half] = (
        keep_own[:, :half] + rcv_a[0].astype(F32) + rcv_a[2].astype(F32)
    ).astype(BF16)
    last_b.wait_recv()
    own[:, half:] = (
        keep_own[:, half:] + rcv_b[0].astype(F32) + rcv_b[2].astype(F32)
    ).astype(BF16)
    down = wire.copy(own.at[pl.ds(cells - edge, edge)], halo_e.at[0], after)
    up = wire.copy(own.at[pl.ds(0, edge)], halo_e.at[1], before)
    ext_e[pl.ds(edge, cells)] = own[...]
    down.wait_recv()
    up.wait_recv()
    zero_e = jnp.zeros((edge, book.shape[1]), BF16)
    ext_e[pl.ds(0, edge)] = jnp.where(block == 0, zero_e, halo_e[0])
    ext_e[pl.ds(edge + cells, edge)] = jnp.where(block == blocks - 1, zero_e, halo_e[1])
    wire.drain()


def front(weights, codebook, cotangent):
    cells, chan = cotangent.shape[0], codebook.shape[1]
    wide = cotangent.shape[1]
    half = chan // 2
    long = cells + 4 * COLS
    vmem = pl.BlockSpec(memory_space=pltpu.VMEM)
    return pl.pallas_call(
        front_kernel,
        out_shape=(
            jax.ShapeDtypeStruct((long, chan), BF16),
            jax.ShapeDtypeStruct((long, wide), BF16),
        ),
        in_specs=[pl.BlockSpec(memory_space=pl.ANY), vmem, vmem],
        out_specs=(vmem, vmem),
        scratch_shapes=[
            pltpu.VMEM((4, cells, weights.shape[1]), BF16),
            pltpu.VMEM((cells, half), F32),
            pltpu.VMEM((cells, half), F32),
            pltpu.VMEM((cells, chan), F32),
            pltpu.VMEM((3, cells, half), BF16),
            pltpu.VMEM((3, cells, half), BF16),
            pltpu.VMEM((3, cells, half), BF16),
            pltpu.VMEM((3, cells, half), BF16),
            pltpu.VMEM((cells, chan), BF16),
            pltpu.VMEM((2, 2 * COLS, chan), BF16),
            pltpu.VMEM((2, 2 * COLS, wide), BF16),
            pltpu.SemaphoreType.DMA((4,)),
            pltpu.SemaphoreType.DMA((10,)),
            pltpu.SemaphoreType.DMA((10,)),
        ],
        compiler_params=pltpu.CompilerParams(collective_id=0, has_side_effects=True),
        name="front",
    )(weights, codebook, cotangent)


def shifted(value, out):
    rows, chan = value.shape
    column = lax.broadcasted_iota(jnp.int32, (rows, chan), 0) & (COLS - 1)
    wide = value.astype(F32)
    zero = jnp.zeros_like(wide)
    out[:, :chan] = jnp.where(column == 0, zero, pltpu.roll(wide, 1, 0)).astype(BF16)
    out[:, chan : 2 * chan] = value.astype(BF16)
    out[:, 2 * chan :] = jnp.where(
        column == COLS - 1, zero, pltpu.roll(wide, rows - 1, 0)
    ).astype(BF16)


def permuted_rows(colour, size):
    row = lax.broadcasted_iota(jnp.int32, (size, 128), 0)
    bit = {}
    for step in range(6):
        bit[(colour + step) % 6] = (row >> (7 - step)) & 1
    core = row >> 8
    x = bit[1] * 2 + (bit[0] ^ bit[1])
    y_hi, y_lo = bit[3], bit[2] ^ bit[3]
    z = bit[5] * 2 + (bit[4] ^ bit[5])
    channel = y_hi * 256 + x * 64 + core * 32 + z * 8 + y_lo * 4 + (row & 3)
    lane = lax.broadcasted_iota(jnp.int32, (size, 128), 1)
    shift = channel - lane
    return jnp.concatenate(
        [(shift == part * 128).astype(F32).astype(BF16) for part in range(size // 128)], axis=1
    )


def segments(colour, start, width, span):
    found = []
    at, stop = (colour - start) * span, (colour - start + 1) * span
    while at < stop:
        tap = at // width
        end = min(stop, (tap + 1) * width)
        found.append((tap, at - tap * width, end - tap * width))
        at = end
    return found


def local_kernel(
    ext_e, ext_c, k_one, k_two, decoded, grad_e, terms,
    e_cat, c_cat, h_cat, g_cat, pre, grad_pre, left,
):
    block = lax.axis_index("space") * 4 + lax.axis_index("code")
    blocks = lax.axis_size("space") * 4
    cells, wide = decoded.shape
    chan = ext_e.shape[1]
    more = cells + 2 * COLS
    span = terms.shape[3]
    shifted(ext_e[...], e_cat)
    shifted(ext_c[...], c_cat)
    value = dot(e_cat[pl.ds(0, more)], k_one[0])
    for tap in (1, 2):
        value += dot(e_cat[pl.ds(tap * COLS, more)], k_one[tap])
    pre[...] = value
    row = lax.broadcasted_iota(jnp.int32, (more, wide), 0)
    outside = ((row < COLS) & (block == 0)) | ((row >= more - COLS) & (block == blocks - 1))
    sigma = 1.0 / (1.0 + jnp.exp(-value))
    shifted(jnp.where(outside, 0.0, value * sigma).astype(BF16), h_cat)
    value = jnp.zeros((more, wide), F32)
    for a in range(3):
        for b in range(3):
            piece = c_cat[pl.ds((2 - a) * COLS, more), pl.ds((2 - b) * wide, wide)]
            value += dot_nt(piece, k_two[a, pl.ds(b * wide, wide)])
    sigma = 1.0 / (1.0 + jnp.exp(-pre[...]))
    value = value * sigma * (1.0 + pre[...] * (1.0 - sigma))
    value = jnp.where(outside, 0.0, value).astype(BF16)
    grad_pre[...] = value
    shifted(value, g_cat)
    value = jnp.zeros((cells, chan), F32)
    for a in range(3):
        for b in range(3):
            piece = g_cat[pl.ds((2 - a) * COLS, cells), pl.ds((2 - b) * wide, wide)]
            value += dot_nt(piece, k_one[a, pl.ds(b * chan, chan)])
    grad_e[...] = value.astype(BF16)
    value = dot(h_cat[pl.ds(0, cells)], k_two[0])
    for tap in (1, 2):
        value += dot(h_cat[pl.ds(tap * COLS, cells)], k_two[tap])
    decoded[...] = value.astype(BF16)
    for colour in range(COLOURS):
        if colour < 2:
            source, cat, first, start, width = grad_pre, e_cat, COLS, 0, 3 * chan
            upstream = source[pl.ds(COLS, cells)]
        else:
            cat, first, start, width = h_cat, 0, 2, 3 * wide
            upstream = ext_c[pl.ds(2 * COLS, cells)]
        left[...] = dot_nt(permuted_rows(colour, wide), upstream).astype(BF16)
        at = 0
        for tap, low, high in segments(colour, start, width, span):
            found = dot(left[...], cat[pl.ds(first + tap * COLS, cells), pl.ds(low, high - low)])
            found = found.astype(BF16)
            terms[0, colour, :, pl.ds(at, high - low)] = found[: wide // 2]
            terms[1, colour, :, pl.ds(at, high - low)] = found[wide // 2 :]
            at += high - low


def local(ext_e, ext_c, kernel_one, kernel_two, cells):
    chan, wide = ext_e.shape[1], ext_c.shape[1]
    long, more = cells + 4 * COLS, cells + 2 * COLS
    span = 9 * (chan + wide) // COLOURS
    vmem = pl.BlockSpec(memory_space=pltpu.VMEM)
    return pl.pallas_call(
        local_kernel,
        out_shape=(
            jax.ShapeDtypeStruct((cells, wide), BF16),
            jax.ShapeDtypeStruct((cells, chan), BF16),
            jax.ShapeDtypeStruct((2, COLOURS, wide // 2, span), BF16),
        ),
        in_specs=[vmem] * 4,
        out_specs=(vmem,) * 3,
        scratch_shapes=[
            pltpu.VMEM((long, 3 * chan), BF16),
            pltpu.VMEM((long, 3 * wide), BF16),
            pltpu.VMEM((more, 3 * wide), BF16),
            pltpu.VMEM((more, 3 * wide), BF16),
            pltpu.VMEM((more, wide), F32),
            pltpu.VMEM((more, wide), BF16),
            pltpu.VMEM((wide, cells), BF16),
        ],
        name="local",
    )(ext_e, ext_c, kernel_one.reshape(3, 3 * chan, wide), kernel_two.reshape(3, 3 * wide, wide))


def back_kernel(
    w_hbm, grad_e, terms, book_out, kern_out,
    wbuf, gath, turned, table, whole, t_zero, t_snd, t_rcv, t_keep,
    r_zero, r_snd1, r_rcv1, r_keep1, r_snd2, r_rcv2, r_keep2, r_snd3, r_rcv3, r_keep3,
    r_snd4, r_rcv4, r_keep4, r_snd5, r_rcv5, r_keep5, r_snd6, r_rcv6, r_keep6,
    load_sem, send_sems, recv_sems,
):
    here = coords()
    core, z = here["core"], here["z"]
    partners, bits = links(here)
    twin = device(here, core=1 - core)
    cells, chan = grad_e.shape
    load = pltpu.make_async_copy(w_hbm, wbuf, load_sem)
    load.start()
    greet([twin] + partners)
    wire = Wire(send_sems, recv_sems)
    zu, zv = flip(z), 3 - z
    to_u, to_v = partners[4], partners[5]
    mid = cells // 2
    top, low = pl.ds(0, mid), pl.ds(mid, mid)

    a_u = wire.copy(grad_e.at[top], gath.at[z, 0], to_u)
    b_v = wire.copy(grad_e.at[low], gath.at[z, 1], to_v)
    zero = [wire.copy(terms.at[1 - core, k], r_zero.at[k], twin) for k in range(COLOURS)]
    a_v = wire.copy(grad_e.at[top], gath.at[z, 0], to_v)
    b_u = wire.copy(grad_e.at[low], gath.at[z, 1], to_u)

    rsnd = [None, r_snd1, r_snd2, r_snd3, r_snd4, r_snd5, r_snd6]
    rrcv = [None, r_rcv1, r_rcv2, r_rcv3, r_rcv4, r_rcv5, r_rcv6]
    rkeep = [None, r_keep1, r_keep2, r_keep3, r_keep4, r_keep5, r_keep6]
    moved = {}

    def reduce_step(k, step):
        dim = (k + step - 1) % 6
        bit, to = bits[dim], partners[dim]
        snd, keep = rsnd[step].at[k], rkeep[step].at[k]
        size = rsnd[step].shape[1]
        if step <= 4:
            if step == 1:
                zero[k].wait_recv()
                ours, theirs = terms.at[core, k], r_zero.at[k]
            else:
                moved[k].wait_recv()
                ours, theirs = rkeep[step - 1].at[k], rrcv[step - 1].at[k]

            def added(which):
                rows = pl.ds(pl.multiple_of(which * size, size), size)
                return (ours[rows].astype(F32) + theirs[rows].astype(F32)).astype(BF16)

            snd[...] = added(1 - bit)
            moved[k] = wire.copy(snd, rrcv[step].at[k], to)
            keep[...] = added(bit)
        else:
            moved[k].wait_recv()
            total = rkeep[step - 1][k].astype(F32) + rrcv[step - 1][k].astype(F32)
            upper, lower = total[:size], total[size:]
            snd[...] = jnp.where(bit == 0, lower, upper)
            moved[k] = wire.copy(snd, rrcv[step].at[k], to)
            keep[...] = jnp.where(bit == 0, upper, lower)

    def reduce_end(k):
        moved[k].wait_recv()
        kern_out[k] = r_keep6[k] + r_rcv6[k]

    for k in range(2):
        reduce_step(k, 1)
    a_u.wait_recv()
    a_far = wire.copy(gath.at[zu, 0], gath.at[zu, 0], to_v)
    b_v.wait_recv()
    b_far = wire.copy(gath.at[zv, 1], gath.at[zv, 1], to_u)
    for k in range(2, COLOURS):
        reduce_step(k, 1)

    gath[z, 0] = grad_e[top]
    gath[z, 1] = grad_e[low]
    row = lax.broadcasted_iota(jnp.int32, (chan, chan), 0)
    column = lax.broadcasted_iota(jnp.int32, (chan, chan), 1)
    unit = (row == column).astype(F32).astype(BF16)

    def turn(which, part):
        at = pl.multiple_of(which * cells + part * mid, mid)
        turned[:, pl.ds(at, mid)] = dot_nt(unit, gath[which, part]).astype(BF16)

    turn(z, 0)
    turn(z, 1)
    turn(zu, 0)
    turn(zv, 1)
    a_v.wait_recv()
    turn(zv, 0)
    b_u.wait_recv()
    turn(zu, 1)
    for k in range(COLOURS):
        reduce_step(k, 2)
    a_far.wait_recv()
    b_far.wait_recv()
    turn(rem(z + 2, 4), 0)
    turn(rem(z + 2, 4), 1)
    load.wait()
    codes = wbuf.shape[1]
    piece = codes // 8
    for n in range(8):
        part = dot(turned[...], wbuf[:, pl.ds(n * piece, piece)])
        table[n // 4, n % 4] = part.T.astype(BF16)

    t_first = [wire.copy(table.at[1 - core, k], t_zero.at[k], twin) for k in range(4)]
    hops = {}
    offsets = {}

    def table_step(k, step):
        dim = (k + step - 1) % 4
        bit, to = bits[dim], partners[dim]
        size = piece >> step
        at = pl.ds(piece - 2 * size, size)
        before = pl.ds(piece - 4 * size, 2 * size)
        if step == 1:
            t_first[k].wait_recv()
            ours, theirs = table.at[core, k], t_zero.at[k]
        else:
            hops[k].wait_recv()
            ours, theirs = t_keep.at[k, before], t_rcv.at[k, before]

        def added(which):
            rows = pl.ds(pl.multiple_of(which * size, size), size)
            return (ours[rows].astype(F32) + theirs[rows].astype(F32)).astype(BF16)

        t_snd[k, at] = added(1 - bit)
        hops[k] = wire.copy(t_snd.at[k, at], t_rcv.at[k, at], to)
        t_keep[k, at] = added(bit)
        offsets[k, step] = (offsets[k, step - 1] if step > 1 else 0) + bit * size

    def table_turn(k):
        hops[k].wait_recv()
        size = piece >> 4
        at = pl.ds(piece - 2 * size, size)
        rows = pl.ds(pl.multiple_of(offsets[k, 4], size), size)
        whole[core, k, rows] = (t_keep[k, at].astype(F32) + t_rcv[k, at].astype(F32)).astype(BF16)

    def table_gather(k, step):
        dim = (k + step - 1) % 4
        size = piece >> step
        if step < 4:
            hops[k].wait_recv()
        rows = pl.ds(pl.multiple_of(offsets[k, step], size), size)
        hops[k] = wire.copy(whole.at[core, k, rows], whole.at[core, k, rows], partners[dim])

    for k in range(4):
        table_step(k, 1)
    for k in range(COLOURS):
        reduce_step(k, 3)
    for k in range(4):
        table_step(k, 2)
    for k in range(COLOURS):
        reduce_step(k, 4)
    for k in range(4):
        table_step(k, 3)
    for k in range(COLOURS):
        reduce_step(k, 5)
    for k in range(4):
        table_step(k, 4)
    for k in range(COLOURS):
        reduce_step(k, 6)
    for k in range(4):
        table_turn(k)
        table_gather(k, 4)
    for k in range(COLOURS):
        reduce_end(k)
    for step in (3, 2, 1):
        for k in range(4):
            table_gather(k, step)
    ends = []
    for k in range(4):
        hops[k].wait_recv()
        ends.append(wire.copy(whole.at[core, k], whole.at[core, k], twin))
        book_out[core, k] = whole[core, k]
    for k in range(4):
        ends[k].wait_recv()
        book_out[1 - core, k] = whole[1 - core, k]
    wire.drain()


def back(weights, grad_e, terms):
    cells, chan = grad_e.shape
    codes = weights.shape[1]
    span, rows = terms.shape[3], terms.shape[2]
    piece = codes // 8
    vmem = pl.BlockSpec(memory_space=pltpu.VMEM)
    stages = []
    for step in range(1, 7):
        kind = BF16 if step <= 4 else F32
        stages += [pltpu.VMEM((COLOURS, rows >> step, span), kind)] * 3
    copies = 6 + COLOURS * 7 + 4 * 10
    return pl.pallas_call(
        back_kernel,
        out_shape=(
            jax.ShapeDtypeStruct((2, 4, piece, chan), BF16),
            jax.ShapeDtypeStruct((COLOURS, rows >> 6, span), F32),
        ),
        in_specs=[pl.BlockSpec(memory_space=pl.ANY), vmem, vmem],
        out_specs=(vmem, vmem),
        scratch_shapes=[
            pltpu.VMEM(weights.shape, BF16),
            pltpu.VMEM((4, 2, cells // 2, chan), BF16),
            pltpu.VMEM((chan, 4 * cells), BF16),
            pltpu.VMEM((2, 4, piece, chan), BF16),
            pltpu.VMEM((2, 4, piece, chan), BF16),
            pltpu.VMEM((4, piece, chan), BF16),
            pltpu.VMEM((4, piece, chan), BF16),
            pltpu.VMEM((4, piece, chan), BF16),
            pltpu.VMEM((4, piece, chan), BF16),
            pltpu.VMEM((COLOURS, rows, span), BF16),
            *stages,
            pltpu.SemaphoreType.DMA,
            pltpu.SemaphoreType.DMA((copies,)),
            pltpu.SemaphoreType.DMA((copies,)),
        ],
        compiler_params=pltpu.CompilerParams(collective_id=1, has_side_effects=True),
        name="back",
    )(weights, grad_e, terms)


def on_device(soft_weights, codebook, kernel_one, kernel_two, cotangent):
    own_rows, breadth, wide = cotangent.shape[1:]
    codes, chan = codebook.shape
    cells = own_rows * breadth
    weights = soft_weights.reshape(-1, codes)
    upstream = cotangent.reshape(cells, wide)
    ext_e, ext_c = front(weights, codebook, upstream)
    decoded, grad_e, terms = local(ext_e, ext_c, kernel_one, kernel_two, cells)
    book, kern = back(weights, grad_e, terms)

    def taps(part, depth):
        lines = part.transpose(1, 0, 2).reshape(part.shape[1], 3, 3, depth)
        return lines.transpose(1, 2, 3, 0)

    return (
        decoded.reshape(cotangent.shape),
        taps(kern[:2], chan),
        taps(kern[2:], wide),
        book.reshape(codes, chan).astype(F32),
    )


def solution(mesh):
    in_specs = (
        P("clip", "space", None, "code"),
        P("code", None),
        P(),
        P(),
        P("clip", ("space", "code"), None, None),
    )
    out_specs = (
        P("clip", ("space", "code"), None, None),
        P(None, None, None, ("space", "code", "clip")),
        P(None, None, None, ("space", "code", "clip")),
        P("code", None),
    )
    return jax.shard_map(
        on_device, mesh=mesh, in_specs=in_specs, out_specs=out_specs, check_vma=False
    )
```
